32 devices in a mesh: gx: 4 (over x, core), gy: 8 (over z, y).
Axes of the slice: x: 2, y: 2, z: 4, core: 2. Of those that a mesh axis runs over, the one named last changes fastest.
Arguments:
- weights: float32 [2, 64, 8, 16, 512], P(None, None, 'gx', 'gy'), may hold values from -6 to 6
- interp: float32 [4, 4, 64, 64], replicated, may hold values from -0.375 to 0.375
- travel: float32 [64, 4096], replicated, may hold values from -3.140625 to 3.140625
- entry_rows: int32 [3, 4, 8, 2048], P(None, 'gx', 'gy'), may hold values from 0 to 4095
- exit_rows: int32 [3, 4, 8, 2048], P(None, 'gx', 'gy'), may hold values from 0 to 4095
Outputs:
- result: float32 [2, 64, 1, 2, 32768], P(None, None, None, None, ('gx', 'gy'))
The draws below stay inside these ranges and needn't reach their ends.
All inputs are finite; a program needn't handle non-finite values.
Results may differ from the reference program's by a relative error of at most 0.0001.
Values sent between devices are 32-bit elements; how exact they have to be, the bound alone decides.
A program may use at most 128 MiB of HBM per device.

```python
import jax
import jax.numpy as jnp
import numpy as np
from jax import lax

Q = 64
TB0 = 512
NROW = 4096
PD = 2048
SX0 = 8
SY0 = 16
N_GX = 4
N_GY = 8


def place_ends(entries, key, low, largest):
    dims = entries.shape
    place = [jax.random.randint(jax.random.fold_in(key, axis), (), 0, dims[axis]) for axis in range(len(dims))]
    entries = entries.at[tuple(place)].set(low)
    longest = dims.index(max(dims))
    place[longest] = (place[longest] + 1) % dims[longest]
    return entries.at[tuple(place)].set(largest)


def shard_levels(rng, shape, shards, low, largest):
    factor_of, own = 1.0, jax.random.fold_in(rng, 6)
    for axis_at, shards_of in shards:
        draws = jnp.exp(jax.random.uniform(jax.random.fold_in(own, axis_at), (shards_of,), jnp.float32, low / len(shards), largest / len(shards)))
        factor_of = factor_of * jnp.repeat(draws, shape[axis_at] // shards_of).reshape([-1 if axis == axis_at else 1 for axis in range(len(shape))])
    return factor_of


def scatter_about(stream_key, shape, deviation, most, pieces=(), kind=jnp.bfloat16):
    factor_of = shard_levels(stream_key, shape, pieces, -0.22, 0.18) if pieces else 1.0
    drawn = jax.random.normal(stream_key, shape, jnp.float32) * deviation * factor_of
    return jnp.minimum(jnp.maximum(drawn, -most), most).astype(kind)


def setup_inputs(seed: int = 0) -> dict:
    keys = jax.random.split(jax.random.key(seed), 6)
    weights = scatter_about(keys[0], (2, Q, SX0, SY0, TB0), 1.0, 6.0, ((2, 4), (3, 8)), jnp.float32)
    interp = scatter_about(keys[1], (4, 4, Q, Q), (4 * Q) ** -0.5, 0.375, (), jnp.float32)
    travel = jnp.clip(jax.random.uniform(keys[2], (Q, NROW), jnp.float32, -3.140625, 3.140625), -3.140625, 3.140625)
    entry_rows = place_ends(jax.random.randint(keys[3], (3, N_GX, N_GY, PD), 0, NROW), jax.random.fold_in(keys[3], 1), 0, NROW - 1).astype(jnp.int32)
    exit_rows = place_ends(jax.random.randint(keys[4], (3, N_GX, N_GY, PD), 0, NROW), jax.random.fold_in(keys[4], 1), 0, NROW - 1).astype(jnp.int32)
    return dict(weights=weights, interp=interp, travel=travel, entry_rows=entry_rows, exit_rows=exit_rows)


highest = lax.Precision.HIGHEST


def rotate(fields, travel, row_index, sign):
    angles = jnp.take(travel, row_index, axis=1)
    cos_part = jnp.cos(angles)
    sin_part = jnp.sin(angles) * sign
    real_part = fields[0]
    imag_part = fields[1]
    return jnp.stack([cos_part * real_part - sin_part * imag_part, sin_part * real_part + cos_part * imag_part])


def combine(fields, interp, level_bit):
    x_bits = (np.arange(N_GX) >> level_bit) & 1
    y_bits = (np.arange(N_GY) >> level_bit) & 1
    target_child = 2 * x_bits[:, None] + y_bits[None, :]
    total = jnp.zeros(fields.shape, jnp.float32)
    for step_x in (0, 1):
        for step_y in (0, 1):
            x_peer = np.arange(N_GX) ^ (step_x << level_bit)
            y_peer = np.arange(N_GY) ^ (step_y << level_bit)
            moved = fields[:, :, x_peer][:, :, :, y_peer]
            source_child = 2 * x_bits[x_peer][:, None] + y_bits[y_peer][None, :]
            matrices = interp[target_child, source_child]
            total = total + jnp.einsum('ijts,rsijp->rtijp', matrices, moved, precision=highest)
    return total


def reference(weights, interp, travel, entry_rows, exit_rows):
    fields = weights.reshape(2, Q, N_GX, 2, N_GY, 2, TB0).transpose(0, 1, 2, 4, 3, 5, 6)
    fields = fields.reshape(2, Q, N_GX, N_GY, 4 * TB0)
    fields = rotate(fields, travel, entry_rows[0], -1.0)
    merged = jnp.einsum('kcts,rsijca->rtijka', interp, fields.reshape(2, Q, N_GX, N_GY, 4, TB0), precision=highest)
    fields = rotate(merged.reshape(2, Q, N_GX, N_GY, 4 * TB0), travel, exit_rows[0], 1.0)
    for section in (1, 2):
        fields = rotate(fields, travel, entry_rows[section], -1.0)
        fields = combine(fields, interp, section - 1)
        fields = rotate(fields, travel, exit_rows[section], 1.0)
    fields = fields.reshape(2, Q, N_GX // 4, 2, 2, N_GY // 4, 2, 2, 4, TB0)
    fields = fields.transpose(0, 1, 2, 5, 9, 8, 4, 7, 3, 6)
    return fields.reshape(2, Q, N_GX // 4, N_GY // 4, 64 * TB0)
```

```python
import functools

import jax
import jax.numpy as jnp
from jax import lax
from jax.experimental import pallas as pl
from jax.experimental.pallas import tpu as pltpu
from jax.sharding import PartitionSpec as P

LANES = 128
f32 = jnp.float32
bf16 = jnp.bfloat16


def sine_cosine(angle):
    half = 0.5 * angle
    square = half * half
    sine = jnp.full_like(half, -1.0 / 39916800)
    for term in (1.0 / 362880, -1.0 / 5040, 1.0 / 120, -1.0 / 6, 1.0):
        sine = sine * square + term
    sine = sine * half
    cosine = jnp.full_like(half, 1.0 / 479001600)
    for term in (-1.0 / 3628800, 1.0 / 40320, -1.0 / 720, 1.0 / 24, -0.5, 1.0):
        cosine = cosine * square + term
    return 2.0 * sine * cosine, 1.0 - 2.0 * sine * sine


def build_table(travel_ref, table_ref):
    blocks = travel_ref.shape[1] // LANES

    def step(block, carry):
        start = pl.multiple_of(block * LANES, LANES)
        sine, cosine = sine_cosine(travel_ref[:, pl.ds(start, LANES)])
        table_ref[pl.ds(start, LANES), :] = jnp.concatenate([cosine, sine], axis=0).T
        return carry

    lax.fori_loop(0, blocks, step, 0, unroll=2)


def build_matrix(interp_ref, high_ref, low_ref):
    children = interp_ref.shape[0]
    for k in range(children):
        for c in range(children):
            block = interp_ref[k, c]
            zero = jnp.zeros_like(block)
            block = jnp.concatenate(
                [jnp.concatenate([block, zero], axis=1), jnp.concatenate([zero, block], axis=1)], axis=0
            )
            high = block.astype(bf16)
            where = (slice(k * LANES, (k + 1) * LANES), slice(c * LANES, (c + 1) * LANES))
            high_ref[where] = high
            low_ref[where] = (block - high.astype(f32)).astype(bf16)


def gather_rows(table_ref, row_of, out_ref, start, rows, unroll=16):
    def step(block, carry):
        base = pl.multiple_of(block * unroll, unroll)
        for u in range(unroll):
            out_ref[pl.ds(start + base + u, 1), :] = table_ref[pl.ds(row_of(base + u), 1), :]
        return carry

    lax.fori_loop(0, rows // unroll, step, 0)


def rotate(fields, rotor, sign):
    first = lax.broadcasted_iota(jnp.int32, fields.shape, 1) < LANES // 2
    swapped = pltpu.roll(rotor, LANES // 2, 1)
    cosine = jnp.where(first, rotor, swapped)
    sine = jnp.where(first, swapped * -sign, rotor * sign)
    return fields * cosine + pltpu.roll(fields, LANES // 2, 1) * sine


def store_split(value, high_ref, low_ref, row, column):
    high = value.astype(bf16)
    where = (pl.ds(row, value.shape[0]), pl.ds(column, LANES))
    high_ref[where] = high
    low_ref[where] = (value - high.astype(f32)).astype(bf16)


def product(high, low, matrix_high, matrix_low):
    dot = functools.partial(
        lax.dot_general, dimension_numbers=(((1,), (1,)), ((), ())), preferred_element_type=f32
    )
    return dot(high, matrix_high) + (dot(low, matrix_high) + dot(high, matrix_low))


def first_kernel(weights_ref, interp_ref, travel_ref, entry_ref, exit_ref, out_ref,
                 table_ref, g0, g1, g2, mh, ml, uh, ul):
    count = out_ref.shape[0] // 4
    build_table(travel_ref, table_ref)
    build_matrix(interp_ref, mh, ml)
    gather_rows(table_ref, lambda p: entry_ref[0, p], g0, 0, 4 * count)
    gather_rows(table_ref, lambda p: exit_ref[0, p], g1, 0, 4 * count)
    gather_rows(table_ref, lambda p: entry_ref[1, p], g2, 0, 4 * count)
    blocks = count // LANES
    for block in range(blocks):
        for c in range(4):
            first = (c // 2) * 2 * blocks + block * 2 + c % 2
            field = weights_ref[pl.ds(first, LANES, stride=4 * blocks), :].T
            field = rotate(field, g0[pl.ds(c * count + block * LANES, LANES), :], -1.0)
            store_split(field, uh, ul, 0, c * LANES)
        merged = product(uh[0:LANES, :], ul[0:LANES, :], mh[...], ml[...])
        for k in range(4):
            rows = pl.ds(k * count + block * LANES, LANES)
            value = rotate(merged[:, k * LANES:(k + 1) * LANES], g1[rows, :], 1.0)
            value = rotate(value, g2[rows, :], -1.0)
            out_ref[pl.ds(block * LANES * 4 + k, LANES, stride=4), :] = value


def level_groups(x_size, y_size, bit):
    groups = []
    for i in range(x_size):
        for j in range(y_size):
            if not (i >> bit & 1 or j >> bit & 1):
                groups.append([
                    (i | (c // 2) << bit) * y_size + (j | (c % 2) << bit) for c in range(4)
                ])
    return groups


def last_kernel(x_size, y_size, state_ref, interp_ref, travel_ref, rows_ref, out_ref,
                table_ref, g0, g1, g2, mh, ml, uh, ul, sorted_ref):
    devices = x_size * y_size
    rows = state_ref.shape[0] // devices
    build_table(travel_ref, table_ref)
    build_matrix(interp_ref, mh, ml)
    for which, g in enumerate((g0, g1, g2)):
        gather_rows(table_ref, lambda p, which=which: rows_ref[which, p], g, 0, devices * rows)
    batch = max(1, 256 // rows)
    x_out, y_out = x_size // 4, y_size // 4

    def level(bit, source_ref, finish):
        groups = level_groups(x_size, y_size, bit)
        for start in range(0, len(groups), batch):
            part = groups[start:start + batch]
            for at, group in enumerate(part):
                for c, slot in enumerate(group):
                    store_split(source_ref[pl.ds(slot * rows, rows), :], uh, ul, at * rows, c * LANES)
            size = len(part) * rows
            merged = product(uh[0:size, :], ul[0:size, :], mh[...], ml[...])
            for at, group in enumerate(part):
                for k, slot in enumerate(group):
                    finish(slot, merged[at * rows:(at + 1) * rows, k * LANES:(k + 1) * LANES])

    def finish_first(slot, value):
        where = pl.ds(slot * rows, rows)
        value = rotate(value, g0[where, :], 1.0)
        state_out[where, :] = rotate(value, g1[where, :], -1.0)

    state_out = g0

    def finish_second(slot, value):
        where = pl.ds(slot * rows, rows)
        value = rotate(value, g2[where, :], 1.0)
        i, j = slot // y_size, slot % y_size
        digits = 8 * (i & 1) + 4 * (j & 1) + 2 * (i >> 1 & 1) + (j >> 1 & 1)
        section = (i // 4) * y_out + j // 4
        sorted_ref[pl.ds(section * rows * 16 + digits, rows, stride=16), :] = value

    level(0, state_ref, finish_first)
    level(1, state_out, finish_second)
    blocks = rows * 16 // LANES
    for sx in range(x_out):
        for sy in range(y_out):
            for block in range(blocks):
                start = (sx * y_out + sy) * rows * 16 + block * LANES
                first = (sx * blocks + block) * y_out + sy
                out_ref[pl.ds(first, LANES, stride=x_out * blocks * y_out), :] = (
                    sorted_ref[pl.ds(start, LANES), :].T
                )


def shards(weights, interp, travel, entry_rows, exit_rows):
    count = weights.shape[-1]
    points = interp.shape[-1]
    x_size = lax.axis_size("gx")
    y_size = lax.axis_size("gy")
    devices = x_size * y_size
    share = count // devices
    pairs = 4 * count
    blocks = count // LANES
    vmem = pl.BlockSpec(memory_space=pltpu.VMEM)
    smem = pl.BlockSpec(memory_space=pltpu.SMEM)
    weight_rows = weights.reshape(2, points, 2, 2, blocks, LANES).transpose(0, 1, 2, 4, 3, 5)
    weight_rows = weight_rows.reshape(2 * points * 4 * blocks, LANES)
    rows_array = pltpu.VMEM((pairs, LANES), f32)
    scratch = [
        pltpu.VMEM((travel.shape[1], LANES), f32),
        rows_array, rows_array, rows_array,
        pltpu.VMEM((4 * LANES, 4 * LANES), bf16),
        pltpu.VMEM((4 * LANES, 4 * LANES), bf16),
        pltpu.VMEM((256, 4 * LANES), bf16),
        pltpu.VMEM((256, 4 * LANES), bf16),
    ]
    params = pltpu.CompilerParams(vmem_limit_bytes=48 * 2**20)
    fields = pl.pallas_call(
        first_kernel,
        out_shape=jax.ShapeDtypeStruct((pairs, LANES), f32),
        in_specs=[vmem, vmem, vmem, smem, smem],
        out_specs=vmem,
        scratch_shapes=scratch,
        compiler_params=params,
    )(weight_rows, interp, travel, entry_rows.reshape(3, pairs), exit_rows.reshape(3, pairs))
    state = lax.all_to_all(
        fields.reshape(devices, 4 * share, LANES), ("gx", "gy"), split_axis=0, concat_axis=0, tiled=True
    ).reshape(pairs, LANES)
    tables = jnp.stack([exit_rows[1, 0, 0], entry_rows[2, 0, 0], exit_rows[2, 0, 0]])
    tables = tables.reshape(3, 4, devices, share).transpose(2, 0, 3, 1).reshape(devices, 3 * share * 4)
    tables = lax.all_to_all(tables, ("gx", "gy"), split_axis=0, concat_axis=0, tiled=True)
    tables = tables.reshape(devices, 3, share * 4).transpose(1, 0, 2).reshape(3, pairs)
    x_out, y_out = x_size // 4, y_size // 4
    out_blocks = 64 * share // LANES
    result = pl.pallas_call(
        functools.partial(last_kernel, x_size, y_size),
        out_shape=jax.ShapeDtypeStruct((2 * points * x_out * y_out * out_blocks, LANES), f32),
        in_specs=[vmem, vmem, vmem, smem],
        out_specs=vmem,
        scratch_shapes=scratch + [rows_array],
        compiler_params=params,
    )(state, interp, travel, tables)
    result = result.reshape(2, points, x_out, out_blocks, y_out, LANES).transpose(0, 1, 2, 4, 3, 5)
    return result.reshape(2, points, x_out, y_out, 64 * share)


def solution(mesh):
    return jax.shard_map(
        shards,
        mesh=mesh,
        in_specs=(
            P(None, None, "gx", "gy", None),
            P(),
            P(),
            P(None, "gx", "gy", None),
            P(None, "gx", "gy", None),
        ),
        out_specs=P(None, None, None, None, ("gx", "gy")),
        check_vma=False,
    )
```

```python
import functools

import jax
import jax.numpy as jnp
from jax import lax
from jax.experimental import pallas as pl
from jax.experimental.pallas import tpu as pltpu
from jax.sharding import PartitionSpec as P

LANES = 128
f32 = jnp.float32
bf16 = jnp.bfloat16


def sine_cosine(angle):
    half = 0.5 * angle
    square = half * half
    sine = jnp.full_like(half, -1.0 / 39916800)
    for term in (1.0 / 362880, -1.0 / 5040, 1.0 / 120, -1.0 / 6, 1.0):
        sine = sine * square + term
    sine = sine * half
    cosine = jnp.full_like(half, 1.0 / 479001600)
    for term in (-1.0 / 3628800, 1.0 / 40320, -1.0 / 720, 1.0 / 24, -0.5, 1.0):
        cosine = cosine * square + term
    return 2.0 * sine * cosine, 1.0 - 2.0 * sine * sine


def build_table(travel_ref, table_ref):
    blocks = travel_ref.shape[1] // LANES

    def step(block, carry):
        start = pl.multiple_of(block * LANES, LANES)
        sine, cosine = sine_cosine(travel_ref[:, pl.ds(start, LANES)])
        table_ref[pl.ds(start, LANES), :] = jnp.concatenate([cosine, sine], axis=0).T
        return carry

    lax.fori_loop(0, blocks, step, 0, unroll=2)


def build_matrix(interp_ref, high_ref, low_ref):
    children = interp_ref.shape[0]
    for k in range(children):
        for c in range(children):
            block = interp_ref[k, c]
            zero = jnp.zeros_like(block)
            block = jnp.concatenate(
                [jnp.concatenate([block, zero], axis=1), jnp.concatenate([zero, block], axis=1)], axis=0
            )
            high = block.astype(bf16)
            where = (slice(k * LANES, (k + 1) * LANES), slice(c * LANES, (c + 1) * LANES))
            high_ref[where] = high
            low_ref[where] = (block - high.astype(f32)).astype(bf16)


def gather_rows(table_ref, row_of, out_ref, start, rows, unroll=16):
    def step(block, carry):
        base = pl.multiple_of(block * unroll, unroll)
        for u in range(unroll):
            out_ref[pl.ds(start + base + u, 1), :] = table_ref[pl.ds(row_of(base + u), 1), :]
        return carry

    lax.fori_loop(0, rows // unroll, step, 0)


def rotate(fields, rotor, sign):
    first = lax.broadcasted_iota(jnp.int32, fields.shape, 1) < LANES // 2
    swapped = pltpu.roll(rotor, LANES // 2, 1)
    cosine = jnp.where(first, rotor, swapped)
    sine = jnp.where(first, swapped * -sign, rotor * sign)
    return fields * cosine + pltpu.roll(fields, LANES // 2, 1) * sine


def store_split(value, high_ref, low_ref, row, column):
    high = value.astype(bf16)
    where = (pl.ds(row, value.shape[0]), pl.ds(column, LANES))
    high_ref[where] = high
    low_ref[where] = (value - high.astype(f32)).astype(bf16)


def product(high, low, matrix_high, matrix_low):
    dot = functools.partial(
        lax.dot_general, dimension_numbers=(((1,), (1,)), ((), ())), preferred_element_type=f32
    )
    return dot(high, matrix_high) + (dot(low, matrix_high) + dot(high, matrix_low))


def level_groups(x_size, y_size, bit):
    groups = []
    for i in range(x_size):
        for j in range(y_size):
            if not (i >> bit & 1 or j >> bit & 1):
                groups.append([
                    (i | (c // 2) << bit) * y_size + (j | (c % 2) << bit) for c in range(4)
                ])
    return groups


def whole_kernel(x_size, y_size, weights_ref, interp_ref, travel_ref, entry_ref, exit_ref, blocks_ref,
                 out_ref, table_ref, e0, e1, e2, g0, g1, g2, mh, ml, uh, ul, send_ref, state_ref,
                 sorted_ref, rows_vmem, rows_smem, row_send, row_recv, data_send, data_recv, smem_sem):
    devices = x_size * y_size
    me = lax.axis_index("gx") * y_size + lax.axis_index("gy")
    pairs = send_ref.shape[0]
    count = pairs // 4
    rows = pairs // devices
    blocks = count // LANES
    per_block = devices // blocks
    batch = max(1, 256 // rows)
    x_out, y_out = x_size // 4, y_size // 4

    def mesh_id(device):
        return (device // y_size, device % y_size)

    barrier = pltpu.get_barrier_semaphore()

    def greet(step, carry):
        pl.semaphore_signal(
            barrier, inc=1, device_id=mesh_id((me + step) % devices),
            device_id_type=pl.DeviceIdType.MESH,
        )
        return carry

    lax.fori_loop(1, devices, greet, 0)
    own_rows = pltpu.make_async_copy(blocks_ref.at[me], rows_vmem.at[me], row_recv.at[me])
    own_rows.start()
    build_table(travel_ref, table_ref)
    build_matrix(interp_ref, mh, ml)
    pl.semaphore_wait(barrier, devices - 1)

    def row_copy(device):
        return pltpu.make_async_remote_copy(
            src_ref=blocks_ref.at[device], dst_ref=rows_vmem.at[me],
            send_sem=row_send.at[device], recv_sem=row_recv.at[me],
            device_id=mesh_id(device), device_id_type=pl.DeviceIdType.MESH,
        )

    def data_copy(device):
        return pltpu.make_async_remote_copy(
            src_ref=send_ref.at[pl.ds(pl.multiple_of(device * rows, rows), rows)],
            dst_ref=state_ref.at[pl.ds(pl.multiple_of(me * rows, rows), rows)],
            send_sem=data_send.at[device], recv_sem=data_recv.at[me],
            device_id=mesh_id(device), device_id_type=pl.DeviceIdType.MESH,
        )

    def each_other(fn):
        def step(at, carry):
            fn((me + at) % devices)
            return carry
        lax.fori_loop(1, devices, step, 0)

    each_other(lambda device: row_copy(device).start())

    own_slot = pl.ds(pl.multiple_of(me * rows, rows), rows)
    own_data = pltpu.make_async_copy(send_ref.at[own_slot], state_ref.at[own_slot], data_recv.at[me])
    for turn in range(blocks):
        block = (me // per_block + turn) % blocks
        for c in range(4):
            base = c * count + block * LANES
            start = c * LANES
            gather_rows(table_ref, lambda p: entry_ref[0, base + p], e0, start, LANES)
            gather_rows(table_ref, lambda p: exit_ref[0, base + p], e1, start, LANES)
            gather_rows(table_ref, lambda p: entry_ref[1, base + p], e2, start, LANES)
        for c in range(4):
            first = (c // 2) * 2 * blocks + block * 2 + c % 2
            field = weights_ref[pl.ds(first, LANES, stride=4 * blocks), :].T
            field = rotate(field, e0[c * LANES:(c + 1) * LANES, :], -1.0)
            store_split(field, uh, ul, 0, c * LANES)
        merged = product(uh[0:LANES, :], ul[0:LANES, :], mh[...], ml[...])
        for k in range(4):
            here = slice(k * LANES, (k + 1) * LANES)
            value = rotate(merged[:, here], e1[here, :], 1.0)
            value = rotate(value, e2[here, :], -1.0)
            send_ref[pl.ds(block * LANES * 4 + k, LANES, stride=4), :] = value
        if turn == 0:
            own_data.start()

        def send(at, carry):
            data_copy(block * per_block + (me + at) % per_block).start()
            return carry

        lax.fori_loop(1 if turn == 0 else 0, per_block, send, 0)

    def rows_arrived(device, carry):
        pltpu.make_async_copy(rows_vmem.at[device], rows_vmem.at[device], row_recv.at[device]).wait()
        return carry

    lax.fori_loop(0, devices, rows_arrived, 0)
    to_smem = pltpu.make_async_copy(rows_vmem, rows_smem, smem_sem)
    to_smem.start()
    to_smem.wait()

    def later_rows(device, carry):
        base = pl.multiple_of(device * rows, rows)
        for which, g in enumerate((g0, g1, g2)):
            for at in range(rows):
                row = rows_smem[device, 0, which * rows + at]
                g[pl.ds(base + at, 1), :] = table_ref[pl.ds(row, 1), :]
        here = pl.ds(base, rows)
        g0[here, :] = rotate(g0[here, :], g1[here, :], -1.0)
        return carry

    lax.fori_loop(0, devices, later_rows, 0)

    def level(bit, source_ref, finish, arrived):
        groups = level_groups(x_size, y_size, bit)
        for start in range(0, len(groups), batch):
            part = groups[start:start + batch]
            for at, group in enumerate(part):
                for c, slot in enumerate(group):
                    arrived(slot)
                    store_split(source_ref[pl.ds(slot * rows, rows), :], uh, ul, at * rows, c * LANES)
            size = len(part) * rows
            merged = product(uh[0:size, :], ul[0:size, :], mh[...], ml[...])
            for at, group in enumerate(part):
                for k, slot in enumerate(group):
                    finish(slot, merged[at * rows:(at + 1) * rows, k * LANES:(k + 1) * LANES])

    def finish_first(slot, value):
        where = pl.ds(slot * rows, rows)
        g1[where, :] = rotate(value, g0[where, :], 1.0)

    def finish_second(slot, value):
        where = pl.ds(slot * rows, rows)
        value = rotate(value, g2[where, :], 1.0)
        i, j = slot // y_size, slot % y_size
        digits = 8 * (i & 1) + 4 * (j & 1) + 2 * (i >> 1 & 1) + (j >> 1 & 1)
        section = (i // 4) * y_out + j // 4
        sorted_ref[pl.ds(section * rows * 16 + digits, rows, stride=16), :] = value

    def data_arrived(slot):
        where = state_ref.at[pl.ds(slot * rows, rows)]
        pltpu.make_async_copy(where, where, data_recv.at[slot]).wait()

    level(0, state_ref, finish_first, data_arrived)
    level(1, g1, finish_second, lambda slot: None)
    out_blocks = rows * 16 // LANES
    for sx in range(x_out):
        for sy in range(y_out):
            for block in range(out_blocks):
                start = (sx * y_out + sy) * rows * 16 + block * LANES
                first = (sx * out_blocks + block) * y_out + sy
                out_ref[pl.ds(first, LANES, stride=x_out * out_blocks * y_out), :] = (
                    sorted_ref[pl.ds(start, LANES), :].T
                )
    each_other(lambda device: row_copy(device).wait_send())
    each_other(lambda device: data_copy(device).wait_send())


def shards(weights, interp, travel, entry_rows, exit_rows):
    count = weights.shape[-1]
    points = interp.shape[-1]
    x_size = lax.axis_size("gx")
    y_size = lax.axis_size("gy")
    devices = x_size * y_size
    share = count // devices
    pairs = 4 * count
    blocks = count // LANES
    vmem = pl.BlockSpec(memory_space=pltpu.VMEM)
    smem = pl.BlockSpec(memory_space=pltpu.SMEM)
    weight_rows = weights.reshape(2, points, 2, 2, blocks, LANES).transpose(0, 1, 2, 4, 3, 5)
    weight_rows = weight_rows.reshape(2 * points * 4 * blocks, LANES)
    tables = jnp.stack([exit_rows[1, 0, 0], entry_rows[2, 0, 0], exit_rows[2, 0, 0]])
    tables = tables.reshape(3, 4, devices, share).transpose(2, 0, 3, 1).reshape(devices, 3 * share * 4)
    width = -(-3 * share * 4 // LANES) * LANES
    tables = jnp.pad(tables, ((0, 0), (0, width - 3 * share * 4))).reshape(devices, 1, width)
    rows_array = pltpu.VMEM((pairs, LANES), f32)
    block_rows = pltpu.VMEM((4 * LANES, LANES), f32)
    matrix = pltpu.VMEM((4 * LANES, 4 * LANES), bf16)
    operand = pltpu.VMEM((256, 4 * LANES), bf16)
    x_out, y_out = x_size // 4, y_size // 4
    out_blocks = 64 * share // LANES
    semaphores = pltpu.SemaphoreType.DMA((devices,))
    result = pl.pallas_call(
        functools.partial(whole_kernel, x_size, y_size),
        out_shape=jax.ShapeDtypeStruct((2 * points * x_out * y_out * out_blocks, LANES), f32),
        in_specs=[vmem, vmem, vmem, smem, smem, vmem],
        out_specs=vmem,
        scratch_shapes=[
            pltpu.VMEM((travel.shape[1], LANES), f32),
            block_rows, block_rows, block_rows,
            rows_array, rows_array, rows_array,
            matrix, matrix, operand, operand,
            rows_array, rows_array, rows_array,
            pltpu.VMEM((devices, 1, width), jnp.int32),
            pltpu.SMEM((devices, 1, width), jnp.int32),
            semaphores, semaphores, semaphores, semaphores,
            pltpu.SemaphoreType.DMA,
        ],
        compiler_params=pltpu.CompilerParams(
            vmem_limit_bytes=48 * 2**20, collective_id=0, has_side_effects=True
        ),
    )(weight_rows, interp, travel, entry_rows.reshape(3, pairs), exit_rows.reshape(3, pairs), tables)
    result = result.reshape(2, points, x_out, out_blocks, y_out, LANES).transpose(0, 1, 2, 4, 3, 5)
    return result.reshape(2, points, x_out, y_out, 64 * share)


def solution(mesh):
    return jax.shard_map(
        shards,
        mesh=mesh,
        in_specs=(
            P(None, None, "gx", "gy", None),
            P(),
            P(),
            P(None, "gx", "gy", None),
            P(None, "gx", "gy", None),
        ),
        out_specs=P(None, None, None, None, ("gx", "gy")),
        check_vma=False,
    )
```

```python
import functools

import jax
import jax.numpy as jnp
from jax import lax
from jax.experimental import pallas as pl
from jax.experimental.pallas import tpu as pltpu
from jax.sharding import PartitionSpec as P

LANES = 128
f32 = jnp.float32
bf16 = jnp.bfloat16


def sine_cosine(angle):
    half = 0.5 * angle
    square = half * half
    sine = jnp.full_like(half, -1.0 / 39916800)
    for term in (1.0 / 362880, -1.0 / 5040, 1.0 / 120, -1.0 / 6, 1.0):
        sine = sine * square + term
    sine = sine * half
    cosine = jnp.full_like(half, 1.0 / 479001600)
    for term in (-1.0 / 3628800, 1.0 / 40320, -1.0 / 720, 1.0 / 24, -0.5, 1.0):
        cosine = cosine * square + term
    return 2.0 * sine * cosine, 1.0 - 2.0 * sine * sine


def build_table(travel_ref, table_ref):
    blocks = travel_ref.shape[1] // LANES

    def step(block, carry):
        start = pl.multiple_of(block * LANES, LANES)
        sine, cosine = sine_cosine(travel_ref[:, pl.ds(start, LANES)])
        table_ref[pl.ds(start, LANES), :] = jnp.concatenate([cosine, sine], axis=0).T
        return carry

    lax.fori_loop(0, blocks, step, 0, unroll=2)


def build_matrix(interp_ref, high_ref, low_ref):
    children = interp_ref.shape[0]
    for k in range(children):
        for c in range(children):
            block = interp_ref[k, c]
            zero = jnp.zeros_like(block)
            block = jnp.concatenate(
                [jnp.concatenate([block, zero], axis=1), jnp.concatenate([zero, block], axis=1)], axis=0
            )
            high = block.astype(bf16)
            where = (slice(k * LANES, (k + 1) * LANES), slice(c * LANES, (c + 1) * LANES))
            high_ref[where] = high
            low_ref[where] = (block - high.astype(f32)).astype(bf16)


def rotate(fields, rotor, sign):
    first = lax.broadcasted_iota(jnp.int32, fields.shape, 1) < LANES // 2
    swapped = pltpu.roll(rotor, LANES // 2, 1)
    cosine = jnp.where(first, rotor, swapped)
    sine = jnp.where(first, swapped * -sign, rotor * sign)
    return fields * cosine + pltpu.roll(fields, LANES // 2, 1) * sine


def store_split(value, high_ref, low_ref, row, column):
    high = value.astype(bf16)
    where = (pl.ds(row, value.shape[0]), pl.ds(column, LANES))
    high_ref[where] = high
    low_ref[where] = (value - high.astype(f32)).astype(bf16)


def product(high, low, matrix_high, matrix_low):
    dot = functools.partial(
        lax.dot_general, dimension_numbers=(((1,), (1,)), ((), ())), preferred_element_type=f32
    )
    return dot(high, matrix_high) + (dot(low, matrix_high) + dot(high, matrix_low))


def level_groups(x_size, y_size, bit):
    groups = []
    for i in range(x_size):
        for j in range(y_size):
            if not (i >> bit & 1 or j >> bit & 1):
                groups.append([
                    (i | (c // 2) << bit) * y_size + (j | (c % 2) << bit) for c in range(4)
                ])
    return groups


def whole_kernel(x_size, y_size, weights_ref, interp_ref, travel_ref, entry_ref, exit_ref, blocks_ref,
                 out_ref, table_ref, e0, e1, e2, g0, g1, g2, mh, ml, uh, ul, send_ref, state_ref,
                 sorted_ref, rows_vmem, rows_smem, row_send, row_recv, data_send, data_recv, smem_sem):
    devices = x_size * y_size
    me = lax.axis_index("gx") * y_size + lax.axis_index("gy")
    pairs = send_ref.shape[0]
    count = pairs // 4
    rows = pairs // devices
    blocks = count // LANES
    per_block = devices // blocks
    batch = max(1, 256 // rows)
    x_out, y_out = x_size // 4, y_size // 4

    def mesh_id(device):
        return (device // y_size, device % y_size)

    barrier = pltpu.get_barrier_semaphore()

    def greet(step, carry):
        pl.semaphore_signal(
            barrier, inc=1, device_id=mesh_id((me + step) % devices),
            device_id_type=pl.DeviceIdType.MESH,
        )
        return carry

    lax.fori_loop(1, devices, greet, 0)
    own_rows = pltpu.make_async_copy(blocks_ref.at[me], rows_vmem.at[me], row_recv.at[me])
    own_rows.start()
    build_table(travel_ref, table_ref)
    build_matrix(interp_ref, mh, ml)
    pl.semaphore_wait(barrier, devices - 1)

    def row_copy(device):
        return pltpu.make_async_remote_copy(
            src_ref=blocks_ref.at[device], dst_ref=rows_vmem.at[me],
            send_sem=row_send.at[device], recv_sem=row_recv.at[me],
            device_id=mesh_id(device), device_id_type=pl.DeviceIdType.MESH,
        )

    def data_copy(device):
        return pltpu.make_async_remote_copy(
            src_ref=send_ref.at[pl.ds(pl.multiple_of(device * rows, rows), rows)],
            dst_ref=state_ref.at[pl.ds(pl.multiple_of(me * rows, rows), rows)],
            send_sem=data_send.at[device], recv_sem=data_recv.at[me],
            device_id=mesh_id(device), device_id_type=pl.DeviceIdType.MESH,
        )

    def each_other(fn):
        def step(at, carry):
            fn((me + at) % devices)
            return carry
        lax.fori_loop(1, devices, step, 0)

    each_other(lambda device: row_copy(device).start())

    own_slot = pl.ds(pl.multiple_of(me * rows, rows), rows)
    own_data = pltpu.make_async_copy(send_ref.at[own_slot], state_ref.at[own_slot], data_recv.at[me])
    for turn in range(blocks):
        own = me // per_block
        block = (own // 2 + turn // 2) % (blocks // 2) * 2 + (own % 2 + turn % 2) % 2

        def early_rows(c, carry, block=block):
            start = pl.multiple_of(c * LANES, LANES)
            at_block = c * blocks + block
            for table, which, out in ((entry_ref, 0, e0), (exit_ref, 0, e1), (entry_ref, 1, e2)):
                for at in range(LANES):
                    row = table[which * 4 * blocks + at_block, 0, at]
                    out[pl.ds(start + at, 1), :] = table_ref[pl.ds(row, 1), :]
            return carry

        lax.fori_loop(0, 4, early_rows, 0)
        for c in range(4):
            first = (c // 2) * 2 * blocks + block * 2 + c % 2
            field = weights_ref[pl.ds(first, LANES, stride=4 * blocks), :].T
            field = rotate(field, e0[c * LANES:(c + 1) * LANES, :], -1.0)
            store_split(field, uh, ul, 0, c * LANES)
        merged = product(uh[0:LANES, :], ul[0:LANES, :], mh[...], ml[...])
        for k in range(4):
            here = slice(k * LANES, (k + 1) * LANES)
            value = rotate(merged[:, here], e1[here, :], 1.0)
            value = rotate(value, e2[here, :], -1.0)
            send_ref[pl.ds(block * LANES * 4 + k, LANES, stride=4), :] = value
        if turn == 0:
            own_data.start()

        def send(at, carry):
            data_copy(block * per_block + (me + at) % per_block).start()
            return carry

        lax.fori_loop(1 if turn == 0 else 0, per_block, send, 0)

    def rows_arrived(device, carry):
        pltpu.make_async_copy(rows_vmem.at[device], rows_vmem.at[device], row_recv.at[device]).wait()
        return carry

    lax.fori_loop(0, devices, rows_arrived, 0)
    to_smem = pltpu.make_async_copy(rows_vmem, rows_smem, smem_sem)
    to_smem.start()
    to_smem.wait()

    def later_rows(device, carry):
        base = pl.multiple_of(device * rows, rows)
        for which, g in enumerate((g0, g1, g2)):
            for at in range(rows):
                row = rows_smem[device, 0, which * rows + at]
                g[pl.ds(base + at, 1), :] = table_ref[pl.ds(row, 1), :]
        here = pl.ds(base, rows)
        g0[here, :] = rotate(g0[here, :], g1[here, :], -1.0)
        return carry

    lax.fori_loop(0, devices, later_rows, 0)

    def level(bit, source_ref, finish):
        groups = level_groups(x_size, y_size, bit)
        for start in range(0, len(groups), batch):
            part = groups[start:start + batch]
            for at, group in enumerate(part):
                for c, slot in enumerate(group):
                    store_split(source_ref[pl.ds(slot * rows, rows), :], uh, ul, at * rows, c * LANES)
            size = len(part) * rows
            merged = product(uh[0:size, :], ul[0:size, :], mh[...], ml[...])
            for at, group in enumerate(part):
                for k, slot in enumerate(group):
                    finish(slot, merged[at * rows:(at + 1) * rows, k * LANES:(k + 1) * LANES])

    def slot_rows(slot):
        return pl.ds(pl.multiple_of(slot * rows, rows), rows)

    x_pairs, y_pairs = x_size // 2, y_size // 2
    for turn in range(x_pairs):
        x_pair = (lax.axis_index("gx") // 2 + turn) % x_pairs
        groups = [
            [(2 * x_pair + c // 2) * y_size + 2 * y_pair + c % 2 for c in range(4)]
            for y_pair in range(y_pairs)
        ]
        for at, group in enumerate(groups):
            for c, slot in enumerate(group):
                arriving = state_ref.at[slot_rows(slot)]
                pltpu.make_async_copy(arriving, arriving, data_recv.at[slot]).wait()
                store_split(state_ref[slot_rows(slot), :], uh, ul, at * rows, c * LANES)
        size = y_pairs * rows
        merged = product(uh[0:size, :], ul[0:size, :], mh[...], ml[...])
        for at, group in enumerate(groups):
            for k, slot in enumerate(group):
                value = merged[at * rows:(at + 1) * rows, k * LANES:(k + 1) * LANES]
                g1[slot_rows(slot), :] = rotate(value, g0[slot_rows(slot), :], 1.0)

    def finish_second(slot, value):
        where = pl.ds(slot * rows, rows)
        value = rotate(value, g2[where, :], 1.0)
        i, j = slot // y_size, slot % y_size
        digits = 8 * (i & 1) + 4 * (j & 1) + 2 * (i >> 1 & 1) + (j >> 1 & 1)
        section = (i // 4) * y_out + j // 4
        sorted_ref[pl.ds(section * rows * 16 + digits, rows, stride=16), :] = value

    level(1, g1, finish_second)
    out_blocks = rows * 16 // LANES
    for sx in range(x_out):
        for sy in range(y_out):
            for block in range(out_blocks):
                start = (sx * y_out + sy) * rows * 16 + block * LANES
                first = (sx * out_blocks + block) * y_out + sy
                out_ref[pl.ds(first, LANES, stride=x_out * out_blocks * y_out), :] = (
                    sorted_ref[pl.ds(start, LANES), :].T
                )
    each_other(lambda device: row_copy(device).wait_send())
    each_other(lambda device: data_copy(device).wait_send())


def shards(weights, interp, travel, entry_rows, exit_rows):
    count = weights.shape[-1]
    points = interp.shape[-1]
    x_size = lax.axis_size("gx")
    y_size = lax.axis_size("gy")
    devices = x_size * y_size
    share = count // devices
    pairs = 4 * count
    blocks = count // LANES
    vmem = pl.BlockSpec(memory_space=pltpu.VMEM)
    smem = pl.BlockSpec(memory_space=pltpu.SMEM)
    weight_rows = weights.reshape(2, points, 2, 2, blocks, LANES).transpose(0, 1, 2, 4, 3, 5)
    weight_rows = weight_rows.reshape(2 * points * 4 * blocks, LANES)
    tables = jnp.stack([exit_rows[1, 0, 0], entry_rows[2, 0, 0], exit_rows[2, 0, 0]])
    tables = tables.reshape(3, 4, devices, share).transpose(2, 0, 3, 1).reshape(devices, 3 * share * 4)
    width = -(-3 * share * 4 // LANES) * LANES
    tables = jnp.pad(tables, ((0, 0), (0, width - 3 * share * 4))).reshape(devices, 1, width)
    rows_array = pltpu.VMEM((pairs, LANES), f32)
    block_rows = pltpu.VMEM((4 * LANES, LANES), f32)
    matrix = pltpu.VMEM((4 * LANES, 4 * LANES), bf16)
    operand = pltpu.VMEM((max(256, y_size // 2 * 4 * share), 4 * LANES), bf16)
    x_out, y_out = x_size // 4, y_size // 4
    out_blocks = 64 * share // LANES
    semaphores = pltpu.SemaphoreType.DMA((devices,))
    result = pl.pallas_call(
        functools.partial(whole_kernel, x_size, y_size),
        out_shape=jax.ShapeDtypeStruct((2 * points * x_out * y_out * out_blocks, LANES), f32),
        in_specs=[vmem, vmem, vmem, smem, smem, vmem],
        out_specs=vmem,
        scratch_shapes=[
            pltpu.VMEM((travel.shape[1], LANES), f32),
            block_rows, block_rows, block_rows,
            rows_array, rows_array, rows_array,
            matrix, matrix, operand, operand,
            rows_array, rows_array, rows_array,
            pltpu.VMEM((devices, 1, width), jnp.int32),
            pltpu.SMEM((devices, 1, width), jnp.int32),
            semaphores, semaphores, semaphores, semaphores,
            pltpu.SemaphoreType.DMA,
        ],
        compiler_params=pltpu.CompilerParams(
            vmem_limit_bytes=48 * 2**20, collective_id=0, has_side_effects=True
        ),
    )(weight_rows, interp, travel, entry_rows.reshape(3 * 4 * blocks, 1, LANES), exit_rows.reshape(3 * 4 * blocks, 1, LANES), tables)
    result = result.reshape(2, points, x_out, out_blocks, y_out, LANES).transpose(0, 1, 2, 4, 3, 5)
    return result.reshape(2, points, x_out, y_out, 64 * share)


def solution(mesh):
    return jax.shard_map(
        shards,
        mesh=mesh,
        in_specs=(
            P(None, None, "gx", "gy", None),
            P(),
            P(),
            P(None, "gx", "gy", None),
            P(None, "gx", "gy", None),
        ),
        out_specs=P(None, None, None, None, ("gx", "gy")),
        check_vma=False,
    )
```

```python
import functools

import jax
import jax.numpy as jnp
from jax import lax
from jax.experimental import pallas as pl
from jax.experimental.pallas import tpu as pltpu
from jax.sharding import PartitionSpec as P

LANES = 128
f32 = jnp.float32
bf16 = jnp.bfloat16


def sine_cosine(angle):
    half = 0.5 * angle
    square = half * half
    sine = jnp.full_like(half, -1.0 / 39916800)
    for term in (1.0 / 362880, -1.0 / 5040, 1.0 / 120, -1.0 / 6, 1.0):
        sine = sine * square + term
    sine = sine * half
    cosine = jnp.full_like(half, 1.0 / 479001600)
    for term in (-1.0 / 3628800, 1.0 / 40320, -1.0 / 720, 1.0 / 24, -0.5, 1.0):
        cosine = cosine * square + term
    return 2.0 * sine * cosine, 1.0 - 2.0 * sine * sine


def build_table(travel_ref, table_ref):
    blocks = travel_ref.shape[1] // LANES

    def step(block, carry):
        start = pl.multiple_of(block * LANES, LANES)
        sine, cosine = sine_cosine(travel_ref[:, pl.ds(start, LANES)])
        table_ref[pl.ds(start, LANES), :] = jnp.concatenate([cosine, sine], axis=0).T
        return carry

    lax.fori_loop(0, blocks, step, 0, unroll=2)


def build_matrix(interp_ref, high_ref, low_ref):
    children = interp_ref.shape[0]
    for k in range(children):
        for c in range(children):
            block = interp_ref[k, c]
            zero = jnp.zeros_like(block)
            block = jnp.concatenate(
                [jnp.concatenate([block, zero], axis=1), jnp.concatenate([zero, block], axis=1)], axis=0
            )
            high = block.astype(bf16)
            where = (slice(k * LANES, (k + 1) * LANES), slice(c * LANES, (c + 1) * LANES))
            high_ref[where] = high
            low_ref[where] = (block - high.astype(f32)).astype(bf16)


def rotate(fields, rotor, sign):
    first = lax.broadcasted_iota(jnp.int32, fields.shape, 1) < LANES // 2
    swapped = pltpu.roll(rotor, LANES // 2, 1)
    cosine = jnp.where(first, rotor, swapped)
    sine = jnp.where(first, swapped * -sign, rotor * sign)
    return fields * cosine + pltpu.roll(fields, LANES // 2, 1) * sine


def store_split(value, high_ref, low_ref, row, column):
    high = value.astype(bf16)
    where = (pl.ds(row, value.shape[0]), pl.ds(column, LANES))
    high_ref[where] = high
    low_ref[where] = (value - high.astype(f32)).astype(bf16)


def product(high, low, matrix_high, matrix_low):
    dot = functools.partial(
        lax.dot_general, dimension_numbers=(((1,), (1,)), ((), ())), preferred_element_type=f32
    )
    return dot(high, matrix_high) + (dot(low, matrix_high) + dot(high, matrix_low))


def level_groups(x_size, y_size, bit):
    groups = []
    for i in range(x_size):
        for j in range(y_size):
            if not (i >> bit & 1 or j >> bit & 1):
                groups.append([
                    (i | (c // 2) << bit) * y_size + (j | (c % 2) << bit) for c in range(4)
                ])
    return groups


def whole_kernel(x_size, y_size, weights_hbm, interp_hbm, travel_hbm, entry_ref, exit_ref, blocks_ref,
                 out_ref, table_ref, e0, e1, e2, g0, g1, g2, mh, ml, uh, ul, send_ref, state_ref,
                 sorted_ref, rows_vmem, rows_smem, row_send, row_recv, data_send, data_recv, smem_sem,
                 weights_ref, interp_ref, travel_ref, load_sem):
    devices = x_size * y_size
    me = lax.axis_index("gx") * y_size + lax.axis_index("gy")
    pairs = send_ref.shape[0]
    count = pairs // 4
    rows = pairs // devices
    blocks = count // LANES
    per_block = devices // blocks
    batch = max(1, 256 // rows)
    x_out, y_out = x_size // 4, y_size // 4

    def mesh_id(device):
        return (device // y_size, device % y_size)

    load_travel = pltpu.make_async_copy(travel_hbm, travel_ref, load_sem.at[0])
    load_interp = pltpu.make_async_copy(interp_hbm, interp_ref, load_sem.at[1])
    load_weights = pltpu.make_async_copy(weights_hbm, weights_ref, load_sem.at[2])
    load_travel.start()
    load_interp.start()
    load_weights.start()
    barrier = pltpu.get_barrier_semaphore()

    def greet(step, carry):
        pl.semaphore_signal(
            barrier, inc=1, device_id=mesh_id((me + step) % devices),
            device_id_type=pl.DeviceIdType.MESH,
        )
        return carry

    lax.fori_loop(1, devices, greet, 0)
    own_rows = pltpu.make_async_copy(blocks_ref.at[me], rows_vmem.at[me], row_recv.at[me])
    own_rows.start()
    load_travel.wait()
    build_table(travel_ref, table_ref)
    load_interp.wait()
    build_matrix(interp_ref, mh, ml)
    load_weights.wait()

    def row_copy(device):
        return pltpu.make_async_remote_copy(
            src_ref=blocks_ref.at[device], dst_ref=rows_vmem.at[me],
            send_sem=row_send.at[device], recv_sem=row_recv.at[me],
            device_id=mesh_id(device), device_id_type=pl.DeviceIdType.MESH,
        )

    def data_copy(device):
        return pltpu.make_async_remote_copy(
            src_ref=send_ref.at[pl.ds(pl.multiple_of(device * rows, rows), rows)],
            dst_ref=state_ref.at[pl.ds(pl.multiple_of(me * rows, rows), rows)],
            send_sem=data_send.at[device], recv_sem=data_recv.at[me],
            device_id=mesh_id(device), device_id_type=pl.DeviceIdType.MESH,
        )

    def each_other(fn):
        def step(at, carry):
            fn((me + at) % devices)
            return carry
        lax.fori_loop(1, devices, step, 0)

    own_slot = pl.ds(pl.multiple_of(me * rows, rows), rows)
    own_data = pltpu.make_async_copy(send_ref.at[own_slot], state_ref.at[own_slot], data_recv.at[me])
    for turn in range(blocks):
        own = me // per_block
        block = (own // 2 + turn // 2) % (blocks // 2) * 2 + (own % 2 + turn % 2) % 2

        def early_rows(c, carry, block=block):
            start = pl.multiple_of(c * LANES, LANES)
            at_block = c * blocks + block
            for table, which, out in ((entry_ref, 0, e0), (exit_ref, 0, e1), (entry_ref, 1, e2)):
                for at in range(LANES):
                    row = table[which * 4 * blocks + at_block, 0, at]
                    out[pl.ds(start + at, 1), :] = table_ref[pl.ds(row, 1), :]
            return carry

        lax.fori_loop(0, 4, early_rows, 0)
        for c in range(4):
            first = (c // 2) * 2 * blocks + block * 2 + c % 2
            field = weights_ref[pl.ds(first, LANES, stride=4 * blocks), :].T
            field = rotate(field, e0[c * LANES:(c + 1) * LANES, :], -1.0)
            store_split(field, uh, ul, 0, c * LANES)
        merged = product(uh[0:LANES, :], ul[0:LANES, :], mh[...], ml[...])
        for k in range(4):
            here = slice(k * LANES, (k + 1) * LANES)
            value = rotate(merged[:, here], e1[here, :], 1.0)
            value = rotate(value, e2[here, :], -1.0)
            send_ref[pl.ds(block * LANES * 4 + k, LANES, stride=4), :] = value
        if turn == 0:
            own_data.start()
            pl.semaphore_wait(barrier, devices - 1)
            each_other(lambda device: row_copy(device).start())

        def send(at, carry):
            data_copy(block * per_block + (me + at) % per_block).start()
            return carry

        lax.fori_loop(1 if turn == 0 else 0, per_block, send, 0)

    def rows_arrived(device, carry):
        pltpu.make_async_copy(rows_vmem.at[device], rows_vmem.at[device], row_recv.at[device]).wait()
        return carry

    lax.fori_loop(0, devices, rows_arrived, 0)
    to_smem = pltpu.make_async_copy(rows_vmem, rows_smem, smem_sem)
    to_smem.start()
    to_smem.wait()

    def later_rows(device, carry):
        base = pl.multiple_of(device * rows, rows)
        for which, g in enumerate((g0, g1, g2)):
            for at in range(rows):
                row = rows_smem[device, 0, which * rows + at]
                g[pl.ds(base + at, 1), :] = table_ref[pl.ds(row, 1), :]
        here = pl.ds(base, rows)
        g0[here, :] = rotate(g0[here, :], g1[here, :], -1.0)
        return carry

    lax.fori_loop(0, devices, later_rows, 0)

    def level(bit, source_ref, finish):
        groups = level_groups(x_size, y_size, bit)
        for start in range(0, len(groups), batch):
            part = groups[start:start + batch]
            for at, group in enumerate(part):
                for c, slot in enumerate(group):
                    store_split(source_ref[pl.ds(slot * rows, rows), :], uh, ul, at * rows, c * LANES)
            size = len(part) * rows
            merged = product(uh[0:size, :], ul[0:size, :], mh[...], ml[...])
            for at, group in enumerate(part):
                for k, slot in enumerate(group):
                    finish(slot, merged[at * rows:(at + 1) * rows, k * LANES:(k + 1) * LANES])

    def slot_rows(slot):
        return pl.ds(pl.multiple_of(slot * rows, rows), rows)

    x_pairs, y_pairs = x_size // 2, y_size // 2
    for turn in range(x_pairs):
        x_pair = (lax.axis_index("gx") // 2 + turn) % x_pairs
        groups = [
            [(2 * x_pair + c // 2) * y_size + 2 * y_pair + c % 2 for c in range(4)]
            for y_pair in range(y_pairs)
        ]
        for at, group in enumerate(groups):
            for c, slot in enumerate(group):
                arriving = state_ref.at[slot_rows(slot)]
                pltpu.make_async_copy(arriving, arriving, data_recv.at[slot]).wait()
                store_split(state_ref[slot_rows(slot), :], uh, ul, at * rows, c * LANES)
        size = y_pairs * rows
        merged = product(uh[0:size, :], ul[0:size, :], mh[...], ml[...])
        for at, group in enumerate(groups):
            for k, slot in enumerate(group):
                value = merged[at * rows:(at + 1) * rows, k * LANES:(k + 1) * LANES]
                g1[slot_rows(slot), :] = rotate(value, g0[slot_rows(slot), :], 1.0)

    def finish_second(slot, value):
        where = pl.ds(slot * rows, rows)
        value = rotate(value, g2[where, :], 1.0)
        i, j = slot // y_size, slot % y_size
        digits = 8 * (i & 1) + 4 * (j & 1) + 2 * (i >> 1 & 1) + (j >> 1 & 1)
        section = (i // 4) * y_out + j // 4
        sorted_ref[pl.ds(section * rows * 16 + digits, rows, stride=16), :] = value

    level(1, g1, finish_second)
    out_blocks = rows * 16 // LANES
    for sx in range(x_out):
        for sy in range(y_out):
            for block in range(out_blocks):
                start = (sx * y_out + sy) * rows * 16 + block * LANES
                first = (sx * out_blocks + block) * y_out + sy
                out_ref[pl.ds(first, LANES, stride=x_out * out_blocks * y_out), :] = (
                    sorted_ref[pl.ds(start, LANES), :].T
                )
    each_other(lambda device: row_copy(device).wait_send())
    each_other(lambda device: data_copy(device).wait_send())


def shards(weights, interp, travel, entry_rows, exit_rows):
    count = weights.shape[-1]
    points = interp.shape[-1]
    x_size = lax.axis_size("gx")
    y_size = lax.axis_size("gy")
    devices = x_size * y_size
    share = count // devices
    pairs = 4 * count
    blocks = count // LANES
    vmem = pl.BlockSpec(memory_space=pltpu.VMEM)
    smem = pl.BlockSpec(memory_space=pltpu.SMEM)
    hbm = pl.BlockSpec(memory_space=pltpu.HBM)
    weight_rows = weights.reshape(2, points, 2, 2, blocks, LANES).transpose(0, 1, 2, 4, 3, 5)
    weight_rows = weight_rows.reshape(2 * points * 4 * blocks, LANES)
    tables = jnp.stack([exit_rows[1, 0, 0], entry_rows[2, 0, 0], exit_rows[2, 0, 0]])
    tables = tables.reshape(3, 4, devices, share).transpose(2, 0, 3, 1).reshape(devices, 3 * share * 4)
    width = -(-3 * share * 4 // LANES) * LANES
    tables = jnp.pad(tables, ((0, 0), (0, width - 3 * share * 4))).reshape(devices, 1, width)
    rows_array = pltpu.VMEM((pairs, LANES), f32)
    block_rows = pltpu.VMEM((4 * LANES, LANES), f32)
    matrix = pltpu.VMEM((4 * LANES, 4 * LANES), bf16)
    operand = pltpu.VMEM((max(256, y_size // 2 * 4 * share), 4 * LANES), bf16)
    x_out, y_out = x_size // 4, y_size // 4
    out_blocks = 64 * share // LANES
    semaphores = pltpu.SemaphoreType.DMA((devices,))
    result = pl.pallas_call(
        functools.partial(whole_kernel, x_size, y_size),
        out_shape=jax.ShapeDtypeStruct((2 * points * x_out * y_out * out_blocks, LANES), f32),
        in_specs=[hbm, hbm, hbm, smem, smem, vmem],
        out_specs=vmem,
        scratch_shapes=[
            pltpu.VMEM((travel.shape[1], LANES), f32),
            block_rows, block_rows, block_rows,
            rows_array, rows_array, rows_array,
            matrix, matrix, operand, operand,
            rows_array, rows_array, rows_array,
            pltpu.VMEM((devices, 1, width), jnp.int32),
            pltpu.SMEM((devices, 1, width), jnp.int32),
            semaphores, semaphores, semaphores, semaphores,
            pltpu.SemaphoreType.DMA,
            pltpu.VMEM(weight_rows.shape, f32),
            pltpu.VMEM(interp.shape, f32),
            pltpu.VMEM(travel.shape, f32),
            pltpu.SemaphoreType.DMA((3,)),
        ],
        compiler_params=pltpu.CompilerParams(
            vmem_limit_bytes=64000000, collective_id=0, has_side_effects=True
        ),
    )(weight_rows, interp, travel, entry_rows.reshape(3 * 4 * blocks, 1, LANES), exit_rows.reshape(3 * 4 * blocks, 1, LANES), tables)
    result = result.reshape(2, points, x_out, out_blocks, y_out, LANES).transpose(0, 1, 2, 4, 3, 5)
    return result.reshape(2, points, x_out, y_out, 64 * share)


def solution(mesh):
    return jax.shard_map(
        shards,
        mesh=mesh,
        in_specs=(
            P(None, None, "gx", "gy", None),
            P(),
            P(),
            P(None, "gx", "gy", None),
            P(None, "gx", "gy", None),
        ),
        out_specs=P(None, None, None, None, ("gx", "gy")),
        check_vma=False,
    )
```

```python
import functools

import jax
import jax.numpy as jnp
from jax import lax
from jax.experimental import pallas as pl
from jax.experimental.pallas import tpu as pltpu
from jax.sharding import PartitionSpec as P

LANES = 128
f32 = jnp.float32
bf16 = jnp.bfloat16


def sine_cosine(angle):
    half = 0.5 * angle
    square = half * half
    sine = jnp.full_like(half, -1.0 / 39916800)
    for term in (1.0 / 362880, -1.0 / 5040, 1.0 / 120, -1.0 / 6, 1.0):
        sine = sine * square + term
    sine = sine * half
    cosine = jnp.full_like(half, 1.0 / 479001600)
    for term in (-1.0 / 3628800, 1.0 / 40320, -1.0 / 720, 1.0 / 24, -0.5, 1.0):
        cosine = cosine * square + term
    return 2.0 * sine * cosine, 1.0 - 2.0 * sine * sine


def build_table(travel_ref, table_ref):
    blocks = travel_ref.shape[1] // LANES

    def step(block, carry):
        start = pl.multiple_of(block * LANES, LANES)
        sine, cosine = sine_cosine(travel_ref[:, pl.ds(start, LANES)])
        table_ref[pl.ds(start, LANES), :] = jnp.concatenate([cosine, sine], axis=0).T
        return carry

    lax.fori_loop(0, blocks, step, 0, unroll=2)


def build_matrix(interp_ref, high_ref, low_ref):
    children = interp_ref.shape[0]
    for k in range(children):
        for c in range(children):
            block = interp_ref[k, c]
            zero = jnp.zeros_like(block)
            block = jnp.concatenate(
                [jnp.concatenate([block, zero], axis=1), jnp.concatenate([zero, block], axis=1)], axis=0
            )
            high = block.astype(bf16)
            where = (slice(k * LANES, (k + 1) * LANES), slice(c * LANES, (c + 1) * LANES))
            high_ref[where] = high
            low_ref[where] = (block - high.astype(f32)).astype(bf16)


def rotate(fields, rotor, sign):
    first = lax.broadcasted_iota(jnp.int32, fields.shape, 1) < LANES // 2
    swapped = pltpu.roll(rotor, LANES // 2, 1)
    cosine = jnp.where(first, rotor, swapped)
    sine = jnp.where(first, swapped * -sign, rotor * sign)
    return fields * cosine + pltpu.roll(fields, LANES // 2, 1) * sine


def store_split(value, high_ref, low_ref, row, column):
    high = value.astype(bf16)
    where = (pl.ds(row, value.shape[0]), pl.ds(column, LANES))
    high_ref[where] = high
    low_ref[where] = (value - high.astype(f32)).astype(bf16)


def product(high, low, matrix_high, matrix_low):
    dot = functools.partial(
        lax.dot_general, dimension_numbers=(((1,), (1,)), ((), ())), preferred_element_type=f32
    )
    return dot(high, matrix_high) + (dot(low, matrix_high) + dot(high, matrix_low))


def level_groups(x_size, y_size, bit):
    groups = []
    for i in range(x_size):
        for j in range(y_size):
            if not (i >> bit & 1 or j >> bit & 1):
                groups.append([
                    (i | (c // 2) << bit) * y_size + (j | (c % 2) << bit) for c in range(4)
                ])
    return groups


def whole_kernel(x_size, y_size, weights_ref, interp_ref, travel_ref, entry_ref, exit_ref, blocks_ref,
                 out_ref, table_ref, e0, e1, e2, g0, g1, g2, mh, ml, uh, ul, send_ref, state_ref,
                 sorted_ref, rows_vmem, rows_smem, row_send, row_recv, data_send, data_recv, smem_sem):
    devices = x_size * y_size
    me = lax.axis_index("gx") * y_size + lax.axis_index("gy")
    pairs = send_ref.shape[0]
    count = pairs // 4
    rows = pairs // devices
    blocks = count // LANES
    per_block = devices // blocks
    batch = max(1, 256 // rows)
    x_out, y_out = x_size // 4, y_size // 4

    def mesh_id(device):
        return (device // y_size, device % y_size)

    barrier = pltpu.get_barrier_semaphore()

    def greet(step, carry):
        pl.semaphore_signal(
            barrier, inc=1, device_id=mesh_id((me + step) % devices),
            device_id_type=pl.DeviceIdType.MESH,
        )
        return carry

    lax.fori_loop(1, devices, greet, 0)
    own_rows = pltpu.make_async_copy(blocks_ref.at[me], rows_vmem.at[me], row_recv.at[me])
    own_rows.start()
    build_table(travel_ref, table_ref)
    build_matrix(interp_ref, mh, ml)

    def row_copy(device):
        return pltpu.make_async_remote_copy(
            src_ref=blocks_ref.at[device], dst_ref=rows_vmem.at[me],
            send_sem=row_send.at[device], recv_sem=row_recv.at[me],
            device_id=mesh_id(device), device_id_type=pl.DeviceIdType.MESH,
        )

    def data_copy(device):
        return pltpu.make_async_remote_copy(
            src_ref=send_ref.at[pl.ds(pl.multiple_of(device * rows, rows), rows)],
            dst_ref=state_ref.at[pl.ds(pl.multiple_of(me * rows, rows), rows)],
            send_sem=data_send.at[device], recv_sem=data_recv.at[me],
            device_id=mesh_id(device), device_id_type=pl.DeviceIdType.MESH,
        )

    def each_other(fn):
        def step(at, carry):
            fn((me + at) % devices)
            return carry
        lax.fori_loop(1, devices, step, 0)

    own_slot = pl.ds(pl.multiple_of(me * rows, rows), rows)
    own_data = pltpu.make_async_copy(send_ref.at[own_slot], state_ref.at[own_slot], data_recv.at[me])
    for turn in range(blocks):
        own = me // per_block
        block = (own // 2 + turn // 2) % (blocks // 2) * 2 + (own % 2 + turn % 2) % 2

        def early_rows(c, carry, block=block):
            start = pl.multiple_of(c * LANES, LANES)
            at_block = c * blocks + block
            for table, which, out in ((entry_ref, 0, e0), (exit_ref, 0, e1), (entry_ref, 1, e2)):
                for at in range(LANES):
                    row = table[which * 4 * blocks + at_block, 0, at]
                    out[pl.ds(start + at, 1), :] = table_ref[pl.ds(row, 1), :]
            return carry

        lax.fori_loop(0, 4, early_rows, 0)
        for c in range(4):
            first = (c // 2) * 2 * blocks + block * 2 + c % 2
            field = weights_ref[pl.ds(first, LANES, stride=4 * blocks), :].T
            field = rotate(field, e0[c * LANES:(c + 1) * LANES, :], -1.0)
            store_split(field, uh, ul, 0, c * LANES)
        merged = product(uh[0:LANES, :], ul[0:LANES, :], mh[...], ml[...])
        for k in range(4):
            here = slice(k * LANES, (k + 1) * LANES)
            value = rotate(merged[:, here], e1[here, :], 1.0)
            value = rotate(value, e2[here, :], -1.0)
            send_ref[pl.ds(block * LANES * 4 + k, LANES, stride=4), :] = value
        if turn == 0:
            own_data.start()
            pl.semaphore_wait(barrier, devices - 1)
            each_other(lambda device: row_copy(device).start())

        def send(at, carry):
            data_copy(block * per_block + (me + at) % per_block).start()
            return carry

        lax.fori_loop(1 if turn == 0 else 0, per_block, send, 0)

    def rows_arrived(device, carry):
        pltpu.make_async_copy(rows_vmem.at[device], rows_vmem.at[device], row_recv.at[device]).wait()
        return carry

    lax.fori_loop(0, devices, rows_arrived, 0)
    to_smem = pltpu.make_async_copy(rows_vmem, rows_smem, smem_sem)
    to_smem.start()
    to_smem.wait()

    def later_rows(device, carry):
        base = pl.multiple_of(device * rows, rows)
        for which, g in enumerate((g0, g1, g2)):
            for at in range(rows):
                row = rows_smem[device, 0, which * rows + at]
                g[pl.ds(base + at, 1), :] = table_ref[pl.ds(row, 1), :]
        here = pl.ds(base, rows)
        g0[here, :] = rotate(g0[here, :], g1[here, :], -1.0)
        return carry

    lax.fori_loop(0, devices, later_rows, 0)

    def level(bit, source_ref, finish):
        groups = level_groups(x_size, y_size, bit)
        for start in range(0, len(groups), batch):
            part = groups[start:start + batch]
            for at, group in enumerate(part):
                for c, slot in enumerate(group):
                    store_split(source_ref[pl.ds(slot * rows, rows), :], uh, ul, at * rows, c * LANES)
            size = len(part) * rows
            merged = product(uh[0:size, :], ul[0:size, :], mh[...], ml[...])
            for at, group in enumerate(part):
                for k, slot in enumerate(group):
                    finish(slot, merged[at * rows:(at + 1) * rows, k * LANES:(k + 1) * LANES])

    def slot_rows(slot):
        return pl.ds(pl.multiple_of(slot * rows, rows), rows)

    x_pairs, y_pairs = x_size // 2, y_size // 2
    for turn in range(x_pairs):
        x_pair = (lax.axis_index("gx") // 2 + turn) % x_pairs
        groups = [
            [(2 * x_pair + c // 2) * y_size + 2 * y_pair + c % 2 for c in range(4)]
            for y_pair in range(y_pairs)
        ]
        for at, group in enumerate(groups):
            for c, slot in enumerate(group):
                arriving = state_ref.at[slot_rows(slot)]
                pltpu.make_async_copy(arriving, arriving, data_recv.at[slot]).wait()
                store_split(state_ref[slot_rows(slot), :], uh, ul, at * rows, c * LANES)
        size = y_pairs * rows
        merged = product(uh[0:size, :], ul[0:size, :], mh[...], ml[...])
        for at, group in enumerate(groups):
            for k, slot in enumerate(group):
                value = merged[at * rows:(at + 1) * rows, k * LANES:(k + 1) * LANES]
                g1[slot_rows(slot), :] = rotate(value, g0[slot_rows(slot), :], 1.0)

    def finish_second(slot, value):
        where = pl.ds(slot * rows, rows)
        value = rotate(value, g2[where, :], 1.0)
        i, j = slot // y_size, slot % y_size
        digits = 8 * (i & 1) + 4 * (j & 1) + 2 * (i >> 1 & 1) + (j >> 1 & 1)
        section = (i // 4) * y_out + j // 4
        sorted_ref[pl.ds(section * rows * 16 + digits, rows, stride=16), :] = value

    level(1, g1, finish_second)
    out_blocks = rows * 16 // LANES
    for sx in range(x_out):
        for sy in range(y_out):
            for block in range(out_blocks):
                start = (sx * y_out + sy) * rows * 16 + block * LANES
                first = (sx * out_blocks + block) * y_out + sy
                out_ref[pl.ds(first, LANES, stride=x_out * out_blocks * y_out), :] = (
                    sorted_ref[pl.ds(start, LANES), :].T
                )
    each_other(lambda device: row_copy(device).wait_send())
    each_other(lambda device: data_copy(device).wait_send())


def shards(weights, interp, travel, entry_rows, exit_rows):
    count = weights.shape[-1]
    points = interp.shape[-1]
    x_size = lax.axis_size("gx")
    y_size = lax.axis_size("gy")
    devices = x_size * y_size
    share = count // devices
    pairs = 4 * count
    blocks = count // LANES
    vmem = pl.BlockSpec(memory_space=pltpu.VMEM)
    smem = pl.BlockSpec(memory_space=pltpu.SMEM)
    weight_rows = weights.reshape(2, points, 2, 2, blocks, LANES).transpose(0, 1, 2, 4, 3, 5)
    weight_rows = weight_rows.reshape(2 * points * 4 * blocks, LANES)
    tables = jnp.stack([exit_rows[1, 0, 0], entry_rows[2, 0, 0], exit_rows[2, 0, 0]])
    tables = tables.reshape(3, 4, devices, share).transpose(2, 0, 3, 1).reshape(devices, 3 * share * 4)
    width = -(-3 * share * 4 // LANES) * LANES
    tables = jnp.pad(tables, ((0, 0), (0, width - 3 * share * 4))).reshape(devices, 1, width)
    rows_array = pltpu.VMEM((pairs, LANES), f32)
    block_rows = pltpu.VMEM((4 * LANES, LANES), f32)
    matrix = pltpu.VMEM((4 * LANES, 4 * LANES), bf16)
    operand = pltpu.VMEM((max(256, y_size // 2 * 4 * share), 4 * LANES), bf16)
    x_out, y_out = x_size // 4, y_size // 4
    out_blocks = 64 * share // LANES
    semaphores = pltpu.SemaphoreType.DMA((devices,))
    result = pl.pallas_call(
        functools.partial(whole_kernel, x_size, y_size),
        out_shape=jax.ShapeDtypeStruct((2 * points * x_out * y_out * out_blocks, LANES), f32),
        in_specs=[vmem, vmem, vmem, smem, smem, vmem],
        out_specs=vmem,
        scratch_shapes=[
            pltpu.VMEM((travel.shape[1], LANES), f32),
            block_rows, block_rows, block_rows,
            rows_array, rows_array, rows_array,
            matrix, matrix, operand, operand,
            rows_array, rows_array, rows_array,
            pltpu.VMEM((devices, 1, width), jnp.int32),
            pltpu.SMEM((devices, 1, width), jnp.int32),
            semaphores, semaphores, semaphores, semaphores,
            pltpu.SemaphoreType.DMA,
        ],
        compiler_params=pltpu.CompilerParams(
            vmem_limit_bytes=48 * 2**20, collective_id=0, has_side_effects=True
        ),
    )(weight_rows, interp, travel, entry_rows.reshape(3 * 4 * blocks, 1, LANES), exit_rows.reshape(3 * 4 * blocks, 1, LANES), tables)
    result = result.reshape(2, points, x_out, out_blocks, y_out, LANES).transpose(0, 1, 2, 4, 3, 5)
    return result.reshape(2, points, x_out, y_out, 64 * share)


def solution(mesh):
    return jax.shard_map(
        shards,
        mesh=mesh,
        in_specs=(
            P(None, None, "gx", "gy", None),
            P(),
            P(),
            P(None, "gx", "gy", None),
            P(None, "gx", "gy", None),
        ),
        out_specs=P(None, None, None, None, ("gx", "gy")),
        check_vma=False,
    )
```
